1024 devices in a mesh: grp: 32 (over x, y_hi, core), blk: 16 (over z), sub: 2 (over y_lo).
Axes of the slice: x: 4, y: 8 (y_hi: 4, y_lo: 2; y = y_hi * 2 + y_lo), z: 16, core: 2. Of those that a mesh axis runs over, the one named last changes fastest.
Arguments:
- clips: bfloat16 [16384, 128, 512], P(('grp', 'blk', 'sub')), may hold values from -6 to 6
- lengths: int32 [16384], P(('grp', 'blk', 'sub')), may hold values from 32 to 128, as said below
- assign: int32 [512, 32], P(('grp', 'blk'), 'sub'), may hold values from 0 to 31, each once within a row
- text: bfloat16 [16384, 1024], P(('grp', 'blk', 'sub')), may hold values from -6 to 6
- positives: int32 [32, 512], P('grp', ('blk', 'sub')), may hold values from 0 to 511, each once within a row
- conv_w: bfloat16 [1536, 512], replicated, may hold values from -0.15625 to 0.15625
- proj_w: bfloat16 [512, 1024], replicated, may hold values from -0.25 to 0.25
- logit_scale: float32 [], replicated, may hold values from 4 to 12
- logit_bias: float32 [], replicated, may hold values from -3 to -1
Outputs:
- audio_grad: float32 [16384, 1024], P(('grp', 'blk', 'sub'))
- text_grad: float32 [16384, 1024], P(('grp', 'blk', 'sub'))
The draws below stay inside these ranges and needn't reach their ends.
Inputs may be any that keep to these rules, and one draw needn't show every extreme that they name: `lengths`: frames at or beyond a clip's length are padding; some clip has 128 frames. `assign`: each row lists each of its pair's 2 * 16 clips once; the first device of the pair takes the first 16 entries. `positives`: each row is a permutation: every text of a group is the match of exactly one audio slot of that group.
All inputs are finite; a program needn't handle non-finite values.
Results may differ from the reference program's by a relative error of at most 0.0045.
Values may be sent and summed in bfloat16 or wider, within the bound.
A program may use at most 32 MiB of HBM per device.

```python
import math
import jax
import jax.numpy as jnp
from jax import lax

CH = 512
E = 1024
ROWS = 16
FRAMES = 128
GROUP_ROWS = 512
BATCH = 16384
PAIRS = 512
N_GRP = 32


def draw_lengths(key, part):
    base = jax.random.randint(jax.random.fold_in(key, 11), (BATCH,), FRAMES // 4, FRAMES + 1)
    spot = jax.random.randint(jax.random.fold_in(key, 12), (), 0, BATCH)
    return jnp.where(jnp.arange(BATCH) == spot, FRAMES, base).astype(jnp.int32)


def draw_clips(key, part):
    frame_key = jax.random.fold_in(key, 21)
    offset_key = jax.random.fold_in(key, 22)
    offset = 1.5 * jax.random.normal(offset_key, (BATCH, 1, CH), jnp.float32)
    frames = jax.random.normal(frame_key, (BATCH, FRAMES, CH), jnp.float32)
    values = frames + offset
    return jnp.clip(values, -6.0, 6.0).astype(jnp.bfloat16)


def shard_levels(rng, dims, split, least, top_value):
    factor_of, own = 1.0, jax.random.fold_in(rng, 6)
    for position, parts in split:
        draws = jnp.exp(jax.random.uniform(jax.random.fold_in(own, position), (parts,), jnp.float32, least / len(split), top_value / len(split)))
        factor_of = factor_of * jnp.repeat(draws, dims[position] // parts).reshape([-1 if axis == position else 1 for axis in range(len(dims))])
    return factor_of


def scatter_about(stream_key, dims, scale, bound, split=(), kind=jnp.bfloat16):
    gain = shard_levels(stream_key, dims, split, -0.22, 0.18) if split else 1.0
    array = jax.random.normal(stream_key, dims, jnp.float32) * scale * gain
    return jnp.minimum(jnp.maximum(array, -bound), bound).astype(kind)


def setup_inputs(seed: int = 0) -> dict:
    seeds = jax.random.split(jax.random.key(seed), 10)
    clips = draw_clips(jax.random.fold_in(seeds[9], 71), 0)
    lengths = draw_lengths(jax.random.fold_in(seeds[9], 71), 0)
    assign = jax.vmap(lambda own: jax.random.permutation(own, 2 * ROWS))(jax.random.split(seeds[2], PAIRS)).reshape((PAIRS, 2 * ROWS)).astype(jnp.int32)
    text = scatter_about(seeds[3], (BATCH, E), 1.0, 6.0, ((0, 1024),))
    positives = jax.vmap(lambda own: jax.random.permutation(own, GROUP_ROWS))(jax.random.split(seeds[4], N_GRP)).reshape((N_GRP, GROUP_ROWS)).astype(jnp.int32)
    conv_w = scatter_about(seeds[5], (3 * CH, CH), (3 * CH) ** -0.5, 0.15625)
    proj_w = scatter_about(seeds[6], (CH, E), CH ** -0.5, 0.25)
    logit_scale = jnp.clip(jnp.exp(jax.random.uniform(seeds[7], (), jnp.float32, math.log(4.0), math.log(12.0))), 4.0, 12.0)
    logit_bias = jnp.clip(jax.random.uniform(seeds[8], (), jnp.float32, -3.0, -1.0), -3.0, -1.0)
    return {"clips": clips, "lengths": lengths, "assign": assign, "text": text, "positives": positives, "conv_w": conv_w, "proj_w": proj_w, "logit_scale": logit_scale, "logit_bias": logit_bias}


def tower(clips, lengths, conv_w, proj_w):
    count_frames = clips.shape[1]
    half = count_frames // 2
    frame_ids = jnp.arange(count_frames, dtype=jnp.int32)
    inside = (frame_ids[None, :] < lengths[:, None])[:, :, None]
    kept = jnp.where(inside, clips, jnp.zeros((), clips.dtype))
    padded = jnp.pad(kept, ((0, 0), (1, 0), (0, 0)))
    stacked = jnp.concatenate([padded[:, 0:count_frames:2], padded[:, 1:count_frames:2], padded[:, 2:count_frames + 1:2]], axis=2)
    hidden = jax.nn.gelu(jnp.dot(stacked.reshape(-1, stacked.shape[2]), conv_w, preferred_element_type=jnp.float32))
    hidden = hidden.reshape(clips.shape[0], half, -1)
    out_ids = jnp.arange(half, dtype=jnp.int32)
    valid = (2 * out_ids[None, :] < lengths[:, None])[:, :, None]
    counts = ((lengths + 1) // 2).astype(jnp.float32)
    pooled = (lax.optimization_barrier(jnp.sum(jnp.where(valid, hidden, jnp.zeros((), hidden.dtype)), axis=1)) / counts[:, None]).astype(jnp.bfloat16)
    projected = jnp.dot(pooled, proj_w, preferred_element_type=jnp.float32)
    return (projected * lax.rsqrt(lax.optimization_barrier(jnp.sum(projected * projected, axis=1, keepdims=True)) + 1e-06)).astype(jnp.bfloat16)

def normalize(values):
    wide = values.astype(jnp.float32)
    return (wide * lax.rsqrt(lax.optimization_barrier(jnp.sum(wide * wide, axis=1, keepdims=True)) + 1e-06)).astype(jnp.bfloat16)

def reference(clips, lengths, assign, text, positives, conv_w, proj_w, logit_scale, logit_bias):
    pair_clips = clips.reshape(PAIRS, 2 * ROWS, FRAMES, CH)
    pair_lengths = lengths.reshape(PAIRS, 2 * ROWS)

    def one_pair(items):
        group_clips, group_lengths, order = items
        embedded = tower(group_clips, group_lengths, conv_w, proj_w)
        return embedded[order]
    audio = lax.map(one_pair, (pair_clips, pair_lengths, assign)).reshape(N_GRP, GROUP_ROWS, E)
    texts = normalize(text).reshape(N_GRP, GROUP_ROWS, E)
    before = jnp.roll(texts, 1, axis=0)

    def one_group(items):
        block, own_text, prev_text, matches = items
        own_logits = logit_scale * jnp.dot(block, own_text.T, preferred_element_type=jnp.float32) + logit_bias
        next_logits = logit_scale * jnp.dot(block, prev_text.T, preferred_element_type=jnp.float32) + logit_bias
        hit = jnp.arange(GROUP_ROWS, dtype=jnp.int32)[None, :] == matches[:, None]
        own_weights = jnp.where(hit, -jax.nn.sigmoid(-own_logits), jax.nn.sigmoid(own_logits)).astype(jnp.bfloat16)
        next_weights = jax.nn.sigmoid(next_logits).astype(jnp.bfloat16)
        audio_part = logit_scale * (jnp.dot(own_weights, own_text, preferred_element_type=jnp.float32) + jnp.dot(next_weights, prev_text, preferred_element_type=jnp.float32))
        own_part = logit_scale * jnp.dot(own_weights.T, block, preferred_element_type=jnp.float32)
        next_part = logit_scale * jnp.dot(next_weights.T, block, preferred_element_type=jnp.float32)
        return (audio_part, own_part, next_part)
    audio_grad, own_part, next_part = lax.map(one_group, (audio, texts, before, positives))
    text_grad = own_part + jnp.roll(next_part, -1, axis=0)
    return (audio_grad.reshape(BATCH, E), text_grad.reshape(BATCH, E))
```

```python
import functools
import math

import jax
import jax.numpy as jnp
from jax import lax
from jax.experimental import pallas as pl
from jax.experimental.pallas import tpu as pltpu
from jax.sharding import PartitionSpec as P

MESH = pl.DeviceIdType.MESH
ROWS = 16
FRAMES = 128
HALF = 64
CH = 512
E = 1024
EXT = 128
TEXT, AUDIO = 0, 1
TEXT_PARENT = {d: d - 1 for d in range(1, 17)}
AUDIO_PARENT = {d: d - 1 for d in range(1, 17)}
CHUNK = 4


def dot_nn(a, b):
    return jnp.dot(a, b, preferred_element_type=jnp.float32)


def dot_nt(a, b):
    return lax.dot_general(a, b, (((1,), (1,)), ((), ())), preferred_element_type=jnp.float32)


def gelu(x):
    inner = math.sqrt(2.0 / math.pi) * (x + 0.044715 * (x * x * x))
    return 0.5 * x * (1.0 + jnp.tanh(inner))


def unit_rows(wide):
    return wide * lax.rsqrt(jnp.sum(wide * wide, axis=1, keepdims=True) + 1e-06)


def weights_of(logits, hit):
    signed = jnp.where(hit, -logits, logits)
    s = jax.nn.sigmoid(signed)
    return jnp.where(hit, -s, s).astype(jnp.bfloat16)


def kernel(
    nz, ng,
    scale_ref, bias_ref, len_ref, assign_ref, pos_ref, text_hbm, clips_hbm, convw_hbm, projw_hbm,
    ag_ref, tg_ref,
    text_v, clips_v, convw_v, projw_v, picked, pool_f, zbuf, praw, pbuf, zx, px, own_a, own_t,
    back_a, got_a, back_t, got_t,
    load_sem, pair_send, pair_recv, ring_send, ring_recv, cross_send, cross_recv,
):
    g, z, s = lax.axis_index("grp"), lax.axis_index("blk"), lax.axis_index("sub")
    other = 1 - s
    up, down = lax.rem(g + 1, ng), lax.rem(g + ng - 1, ng)
    far = nz // 2
    parents = {TEXT: TEXT_PARENT, AUDIO: AUDIO_PARENT}
    bufs = {TEXT: zbuf, AUDIO: pbuf}
    scale, bias = scale_ref[0], bias_ref[0]

    def at_z(offset):
        return lax.rem(z + offset + 2 * nz, nz)

    n_chunks = ROWS // CHUNK
    loads = {"text": pltpu.make_async_copy(text_hbm, text_v, load_sem.at[0])}
    loads["conv"] = pltpu.make_async_copy(convw_hbm, convw_v, load_sem.at[1])
    loads["proj"] = pltpu.make_async_copy(projw_hbm, projw_v, load_sem.at[2])
    for i in range(n_chunks):
        part = pl.ds(i * CHUNK, CHUNK)
        loads[i] = pltpu.make_async_copy(clips_hbm.at[part], clips_v.at[part], load_sem.at[3 + i])
    for name in ("text", 0, "conv", *range(1, n_chunks), "proj"):
        loads[name].start()

    jumps = sorted({d - p for table in parents.values() for d, p in table.items() if d <= far})
    barrier = pltpu.get_barrier_semaphore()
    greeted = [{"sub": other}, {"grp": up}, {"grp": down}]
    for jump in jumps:
        greeted += [{"blk": at_z(jump)}, {"blk": at_z(-jump)}]
    for device in greeted:
        pl.semaphore_signal(barrier, inc=1, device_id=device, device_id_type=MESH)

    loads["text"].wait()
    zt = unit_rows(text_v[...].astype(jnp.float32)).astype(jnp.bfloat16)
    diagonal = lax.broadcasted_iota(jnp.int32, (ROWS, ROWS), 0) == lax.broadcasted_iota(
        jnp.int32, (ROWS, ROWS), 1
    )

    def column(row):
        return jnp.sum(jnp.where(diagonal, row, 0), axis=1, keepdims=True)

    pos_col = column(pos_ref[...])
    assign_col = column(assign_ref[...])
    lane = lax.broadcasted_iota(jnp.int32, (ROWS, EXT), 1)
    extra = jnp.where(lane == 0, pos_col >> 8, jnp.where(lane == 1, pos_col & 255, 0))
    extra = jnp.where(lane == 2, assign_col, extra)
    zbuf[z, s, :, pl.ds(0, E)] = zt
    zbuf[z, s, :, pl.ds(E, EXT)] = extra.astype(jnp.float32).astype(jnp.bfloat16)

    pl.semaphore_wait(barrier, len(greeted))

    sent = []

    def ring_copy(kind, sign, d, r):
        hop = d - parents[kind][d]
        here = bufs[kind].at[at_z(-sign * (d - hop)), s if r == 0 else other]
        return pltpu.make_async_remote_copy(
            src_ref=here, dst_ref=here,
            send_sem=ring_send.at[kind, (1 - sign) // 2, d - 1, r],
            recv_sem=ring_recv.at[kind, (1 - sign) // 2, d - 1, r],
            device_id={"blk": at_z(sign * hop)}, device_id_type=MESH,
        )

    def travels(sign, d, r):
        return d < far or (d == far and r == (1 - sign) // 2)

    def pass_on(kind, d, r, signs=(1, -1)):
        for child in range(far, d, -1):
            if parents[kind][child] == d:
                for sign in signs:
                    if travels(sign, child, r):
                        copy = ring_copy(kind, sign, child, r)
                        copy.start()
                        sent.append(copy)

    def arrived(kind, sign, d, r):
        landed = bufs[kind].at[at_z(-sign * d), s if r == 0 else other]
        pltpu.make_async_remote_copy(
            src_ref=landed, dst_ref=landed,
            send_sem=ring_send.at[kind, (1 - sign) // 2, d - 1, r],
            recv_sem=ring_recv.at[kind, (1 - sign) // 2, d - 1, r],
            device_id={"blk": at_z(sign)}, device_id_type=MESH,
        ).wait_recv()

    def relay(kind, d):
        for r in (0, 1):
            for sign in (1, -1):
                if travels(sign, d, r):
                    arrived(kind, sign, d, r)
                    pass_on(kind, d, r, (sign,))

    def remote(src, dst, send, recv, device):
        return pltpu.make_async_remote_copy(
            src_ref=src, dst_ref=dst, send_sem=send, recv_sem=recv, device_id=device,
            device_id_type=MESH,
        )

    def launch(copy):
        copy.start()
        sent.append(copy)
        return copy

    pass_on(TEXT, 0, 0)
    mine = zbuf.at[z, s]
    text_pair = launch(remote(mine, mine, pair_send.at[0], pair_recv.at[0], {"sub": other}))
    text_up = launch(remote(mine, zx, cross_send.at[0], cross_recv.at[0], {"grp": up}))

    frame = lax.broadcasted_iota(jnp.int32, (3 * HALF, FRAMES), 1)
    place = lax.broadcasted_iota(jnp.int32, (3 * HALF, FRAMES), 0)
    tap = (place >= HALF).astype(jnp.int32) + (place >= 2 * HALF).astype(jnp.int32)
    wanted = 2 * (place - HALF * tap) + tap - 1
    out_id = lax.broadcasted_iota(jnp.int32, (HALF, CH), 0)

    def tower_chunk(i):
        loads[i].wait()
        for c in range(CHUNK):
            clip = i * CHUNK + c
            length = len_ref[clip]
            choose = jnp.where((wanted == frame) & (frame < length), 1.0, 0.0).astype(jnp.bfloat16)
            rows = dot_nn(choose, clips_v[clip]).astype(jnp.bfloat16)
            for k in range(3):
                picked[pl.ds(c * HALF, HALF), pl.ds(k * CH, CH)] = rows[k * HALF : (k + 1) * HALF]
        if i == 0:
            loads["conv"].wait()
        hidden = gelu(dot_nn(picked[...], convw_v[...]))
        for c in range(CHUNK):
            clip = i * CHUNK + c
            length = len_ref[clip]
            kept = jnp.where(2 * out_id < length, hidden[c * HALF : (c + 1) * HALF], 0.0)
            total = jnp.sum(kept, axis=0, keepdims=True)
            count = jnp.full((1, CH), (length + 1) >> 1, jnp.int32).astype(jnp.float32)
            pool_f[pl.ds(clip, 1), :] = total / count

    def pair_texts():
        text_pair.wait_recv()
        pass_on(TEXT, 0, 1)

    tower_chunk(0)
    tower_chunk(1)
    pair_texts()
    tower_chunk(2)
    relay(TEXT, 1)
    tower_chunk(3)

    praw[s] = pool_f[...].astype(jnp.bfloat16)
    audio_pair = launch(
        remote(praw.at[s], praw.at[s], pair_send.at[1], pair_recv.at[1], {"sub": other})
    )
    relay(TEXT, 2)
    loads["proj"].wait()
    audio_pair.wait_recv()
    slot_clip = zbuf[z, :, :, pl.ds(E, EXT)].reshape(2 * ROWS, EXT).astype(jnp.float32)[:, 2:3]
    clip_id = lax.broadcasted_iota(jnp.int32, (2 * ROWS, 2 * ROWS), 1).astype(jnp.float32)
    order = jnp.where(slot_clip == clip_id, 1.0, 0.0).astype(jnp.bfloat16)
    slots = dot_nn(order, praw[...].reshape(2 * ROWS, CH)).astype(jnp.bfloat16)
    pbuf[z] = slots.reshape(2, ROWS, CH)
    pass_on(AUDIO, 0, 0)
    pass_on(AUDIO, 0, 1)
    mine_p = pbuf.at[z, s]
    audio_down = launch(remote(mine_p, px, cross_send.at[1], cross_recv.at[1], {"grp": down}))

    text_up.wait_recv()
    mine_first = lax.broadcasted_iota(jnp.int32, (2 * ROWS, 1), 0)
    own_texts = jnp.concatenate([zbuf[z, s, :, pl.ds(0, E)], zx[:, pl.ds(0, E)]], axis=0)
    text_id = jnp.where(mine_first < ROWS, (2 * z + s) * ROWS + mine_first, -1).astype(jnp.float32)
    ext_lane = lax.broadcasted_iota(jnp.int32, (2 * ROWS, EXT), 1)
    pos_pick = jnp.where(ext_lane == 0, 256.0, jnp.where(ext_lane == 1, 1.0, 0.0))
    pos_pick = pos_pick.astype(jnp.bfloat16)

    def embed(pooled):
        return unit_rows(dot_nn(pooled, projw_v[...])).astype(jnp.bfloat16)

    own_t[...] = jnp.zeros_like(own_t)

    def text_side(pooled, extras):
        audio = embed(pooled)
        logits = scale * dot_nt(own_texts, audio) + bias
        hit = dot_nt(pos_pick, extras) == text_id
        own_t[...] += dot_nn(weights_of(logits, hit), audio)

    def blocks_of(where):
        pooled = [pbuf[at_z(o)].reshape(2 * ROWS, CH) for o in where]
        extras = [zbuf[at_z(o), :, :, pl.ds(E, EXT)].reshape(2 * ROWS, EXT) for o in where]
        if len(where) == 1:
            return pooled[0], extras[0]
        return jnp.concatenate(pooled, axis=0), jnp.concatenate(extras, axis=0)

    def audio_side():
        audio_down.wait_recv()
        rows = jnp.concatenate([pbuf[z, s], px[...]], axis=0)
        audio = embed(rows)
        texts = zbuf[:, :, :, pl.ds(0, E)].reshape(nz * 2 * ROWS, E)
        logits = scale * dot_nt(audio, texts) + bias
        pos = jnp.concatenate([pos_col, jnp.full((ROWS, 1), -1, jnp.int32)], axis=0)
        hit = lax.broadcasted_iota(jnp.int32, logits.shape, 1) == pos
        own_a[...] = scale * dot_nn(weights_of(logits, hit), texts)
        back_a[...] = own_a[pl.ds(ROWS, ROWS), :].astype(jnp.bfloat16)
        return launch(remote(back_a, got_a, cross_send.at[2], cross_recv.at[2], {"grp": up}))

    lead = 2
    text_side(*blocks_of([0]))
    audio_up = None
    for d in range(1, far + 1):
        if d + lead <= far:
            relay(TEXT, d + lead)
        relay(AUDIO, d)
        text_side(*blocks_of([d, -d] if d < far else [d]))
        if d + lead == far + 1 or (audio_up is None and d == far):
            audio_up = audio_side()

    own_t[...] = scale * own_t[...]
    back_t[...] = own_t[pl.ds(ROWS, ROWS), :].astype(jnp.bfloat16)
    text_down = launch(remote(back_t, got_t, cross_send.at[3], cross_recv.at[3], {"grp": down}))

    audio_up.wait_recv()
    ag_ref[...] = own_a[pl.ds(0, ROWS), :] + got_a[...].astype(jnp.float32)
    text_down.wait_recv()
    tg_ref[...] = own_t[pl.ds(0, ROWS), :] + got_t[...].astype(jnp.float32)
    for copy in sent:
        copy.wait_send()


def on_device(nz, ng, clips, lengths, assign, text, positives, conv_w, proj_w, logit_scale, logit_bias):
    far = nz // 2
    smem = pl.BlockSpec(memory_space=pltpu.SMEM)
    vmem = pl.BlockSpec(memory_space=pltpu.VMEM)
    hbm = pl.BlockSpec(memory_space=pl.ANY)
    bf16, f32, dma = jnp.bfloat16, jnp.float32, pltpu.SemaphoreType.DMA
    out = jax.ShapeDtypeStruct((ROWS, E), f32)
    return pl.pallas_call(
        functools.partial(kernel, nz, ng),
        out_shape=(out, out),
        in_specs=[smem, smem, smem, vmem, vmem, hbm, hbm, hbm, hbm],
        out_specs=(vmem, vmem),
        scratch_shapes=[
            pltpu.VMEM((ROWS, E), bf16),
            pltpu.VMEM((ROWS, FRAMES, CH), bf16),
            pltpu.VMEM((3 * CH, CH), bf16),
            pltpu.VMEM((CH, E), bf16),
            pltpu.VMEM((CHUNK * HALF, 3 * CH), bf16),
            pltpu.VMEM((ROWS, CH), f32),
            pltpu.VMEM((nz, 2, ROWS, E + EXT), bf16),
            pltpu.VMEM((2, ROWS, CH), bf16),
            pltpu.VMEM((nz, 2, ROWS, CH), bf16),
            pltpu.VMEM((ROWS, E + EXT), bf16),
            pltpu.VMEM((ROWS, CH), bf16),
            pltpu.VMEM((2 * ROWS, E), f32),
            pltpu.VMEM((2 * ROWS, E), f32),
            pltpu.VMEM((ROWS, E), bf16),
            pltpu.VMEM((ROWS, E), bf16),
            pltpu.VMEM((ROWS, E), bf16),
            pltpu.VMEM((ROWS, E), bf16),
            dma((3 + ROWS // CHUNK,)),
            dma((2,)),
            dma((2,)),
            dma((2, 2, far, 2)),
            dma((2, 2, far, 2)),
            dma((4,)),
            dma((4,)),
        ],
        compiler_params=pltpu.CompilerParams(
            collective_id=0, has_side_effects=True, vmem_limit_bytes=67043328
        ),
        name="contrastive_step",
    )(
        logit_scale.reshape(1), logit_bias.reshape(1), lengths, assign, positives, text, clips,
        conv_w, proj_w,
    )


def solution(mesh):
    in_specs = (
        P(("grp", "blk", "sub"), None, None),
        P(("grp", "blk", "sub")),
        P(("grp", "blk"), "sub"),
        P(("grp", "blk", "sub"), None),
        P("grp", ("blk", "sub")),
        P(),
        P(),
        P(),
        P(),
    )
    out_specs = (P(("grp", "blk", "sub"), None), P(("grp", "blk", "sub"), None))
    body = functools.partial(on_device, mesh.shape["blk"], mesh.shape["grp"])
    return jax.shard_map(body, mesh=mesh, in_specs=in_specs, out_specs=out_specs, check_vma=False)
```

```python
import functools
import math

import jax
import jax.numpy as jnp
from jax import lax
from jax.experimental import pallas as pl
from jax.experimental.pallas import tpu as pltpu
from jax.sharding import PartitionSpec as P

MESH = pl.DeviceIdType.MESH
ROWS = 16
FRAMES = 128
HALF = 64
CH = 512
E = 1024
EXT = 128
TEXT, AUDIO = 0, 1
TEXT_PARENT = {d: (d - 1) // 2 * 2 for d in range(1, 9)}
AUDIO_PARENT = {d: (d - 1) // 4 * 4 for d in range(1, 9)}
CHUNK = 4
EARLY = 2


def dot_nn(a, b):
    return jnp.dot(a, b, preferred_element_type=jnp.float32)


def dot_nt(a, b):
    return lax.dot_general(a, b, (((1,), (1,)), ((), ())), preferred_element_type=jnp.float32)


def gelu(x):
    inner = math.sqrt(2.0 / math.pi) * (x + 0.044715 * (x * x * x))
    return 0.5 * x * (1.0 + jnp.tanh(inner))


def unit_rows(wide):
    return wide * lax.rsqrt(jnp.sum(wide * wide, axis=1, keepdims=True) + 1e-06)


def weights_of(logits, hit):
    signed = jnp.where(hit, -logits, logits)
    s = jax.nn.sigmoid(signed)
    return jnp.where(hit, -s, s).astype(jnp.bfloat16)


def kernel(
    nz, ng,
    scale_ref, bias_ref, len_ref, assign_ref, pos_ref, text_hbm, clips_hbm, convw_hbm, projw_hbm,
    own_a, own_t, got_a, got_t,
    text_v, clips_v, convw_v, projw_v, picked, pool_f, zbuf, abuf, text_rows, pooled, slot_rows, info,
    part_a, part_t, back_a, back_t,
    load_sem, pair_send, pair_recv, ring_send, ring_recv, rows_send, rows_recv, part_send, part_recv,
):
    g, z, s = lax.axis_index("grp"), lax.axis_index("blk"), lax.axis_index("sub")
    other = 1 - s
    up, down = lax.rem(g + 1, ng), lax.rem(g + ng - 1, ng)
    far = nz // 2
    parents = {TEXT: TEXT_PARENT, AUDIO: AUDIO_PARENT}
    bufs = {TEXT: zbuf, AUDIO: abuf}
    scale, bias = scale_ref[0], bias_ref[0]
    sign1 = jnp.where(z < far, -1, 1)
    signs = (sign1, -sign1)

    def at_z(offset):
        return lax.rem(z + offset + 2 * nz, nz)

    n_chunks = ROWS // CHUNK
    loads = {"text": pltpu.make_async_copy(text_hbm, text_v, load_sem.at[0])}
    loads["conv"] = pltpu.make_async_copy(convw_hbm, convw_v, load_sem.at[1])
    loads["proj"] = pltpu.make_async_copy(projw_hbm, projw_v, load_sem.at[2])
    for i in range(n_chunks):
        part = pl.ds(i * CHUNK, CHUNK)
        loads[i] = pltpu.make_async_copy(clips_hbm.at[part], clips_v.at[part], load_sem.at[3 + i])
    for name in ("text", 0, "conv", *range(1, n_chunks), "proj"):
        loads[name].start()

    jumps = {d - p for table in parents.values() for d, p in table.items() if d <= far}
    barrier = pltpu.get_barrier_semaphore()
    greeted = [{"sub": other}]
    greeted += [{"grp": near_group, "sub": h} for near_group in (up, down) for h in (0, 1)]
    for place in sorted({j % nz for j in jumps} | {-j % nz for j in jumps}):
        greeted.append({"blk": at_z(place)})
    for device in greeted:
        pl.semaphore_signal(barrier, inc=1, device_id=device, device_id_type=MESH)

    sent = []

    def remote(src, dst, send, recv, device):
        return pltpu.make_async_remote_copy(
            src_ref=src, dst_ref=dst, send_sem=send, recv_sem=recv, device_id=device,
            device_id_type=MESH,
        )

    def launch(copy):
        copy.start()
        sent.append(copy)
        return copy

    def ring_copy(kind, sign, d, back):
        hop = d - parents[kind][d]
        here = bufs[kind].at[at_z(-sign * (d if back else d - hop))]
        way = (1 - sign) // 2
        return remote(
            here, here, ring_send.at[kind, way, d - 1], ring_recv.at[kind, way, d - 1],
            {"blk": at_z(sign * hop)},
        )

    def arrive(kind, sign, d):
        ring_copy(kind, sign, d, True).wait_recv()

    def pass_on(kind, sign, d):
        for child in range(far - 1, d, -1):
            if parents[kind][child] == d:
                launch(ring_copy(kind, sign, child, False))

    def pass_half_way(kind, d):
        if parents[kind][far] == d:
            launch(ring_copy(kind, -1, far, False))

    def set_out(kind):
        pass_half_way(kind, 0)
        for sign in signs:
            pass_on(kind, sign, 0)

    relays = {k: sorted({p for d, p in t.items() if d <= far and p > 0}) for k, t in parents.items()}
    leaves = {k: [d for d in range(1, far) if d not in relays[k]] for k in parents}

    def relay(kind):
        for d in relays[kind]:
            for sign in signs:
                arrive(kind, sign, d)
                pass_on(kind, sign, d)
            pass_half_way(kind, d)

    def leaf(kind, index):
        for d in leaves[kind]:
            arrive(kind, signs[index], d)

    def both_subs(src, dst, sems, group):
        for h in (0, 1):
            launch(
                remote(
                    src, dst, rows_send.at[sems, h], rows_recv.at[sems, s], {"grp": group, "sub": h}
                )
            )

    def both_came(dst, sems):
        for h in (0, 1):
            here = dst.at[2 + h]
            remote(
                here, here, rows_send.at[sems, h], rows_recv.at[sems, h], {"grp": up, "sub": h}
            ).wait_recv()

    def hand_back(src, dst, sems, group):
        launch(
            remote(src.at[other], dst.at[0], part_send.at[sems, 0], part_recv.at[sems, 0], {"sub": other})
        )
        for h in (0, 1):
            launch(
                remote(
                    src.at[2 + h], dst.at[1 + s], part_send.at[sems, 1 + h],
                    part_recv.at[sems, 1 + s], {"grp": group, "sub": h},
                )
            )

    def handed_back(dst, sems):
        for i in range(3):
            here = dst.at[i]
            remote(
                here, here, part_send.at[sems, i], part_recv.at[sems, i], {"sub": other}
            ).wait_recv()

    loads["text"].wait()
    zt = unit_rows(text_v[...].astype(jnp.float32)).astype(jnp.bfloat16)
    zbuf[z] = zt
    text_rows[s] = zt
    info[s, pl.ds(0, 1), pl.ds(0, ROWS)] = assign_ref[...]
    info[s, pl.ds(1, 1), pl.ds(0, ROWS)] = pos_ref[...]
    sub_id = lax.broadcasted_iota(jnp.int32, (ROWS, ROWS), 0)
    lane_id = lax.broadcasted_iota(jnp.int32, (ROWS, ROWS), 1)

    def column(row):
        return jnp.sum(jnp.where(sub_id == lane_id, row, 0), axis=1, keepdims=True)

    frame = lax.broadcasted_iota(jnp.int32, (3 * HALF, FRAMES), 1)
    place = lax.broadcasted_iota(jnp.int32, (3 * HALF, FRAMES), 0)
    tap = (place >= HALF).astype(jnp.int32) + (place >= 2 * HALF).astype(jnp.int32)
    wanted = 2 * (place - HALF * tap) + tap - 1
    out_id = lax.broadcasted_iota(jnp.int32, (HALF, CH), 0)

    def tower_chunk(i):
        loads[i].wait()
        for c in range(CHUNK):
            clip = i * CHUNK + c
            length = len_ref[clip]
            choose = jnp.where((wanted == frame) & (frame < length), 1.0, 0.0).astype(jnp.bfloat16)
            rows = dot_nn(choose, clips_v[clip]).astype(jnp.bfloat16)
            for k in range(3):
                picked[pl.ds(c * HALF, HALF), pl.ds(k * CH, CH)] = rows[k * HALF : (k + 1) * HALF]
        if i == 0:
            loads["conv"].wait()
        hidden = gelu(dot_nn(picked[...], convw_v[...]))
        for c in range(CHUNK):
            clip = i * CHUNK + c
            length = len_ref[clip]
            kept = jnp.where(2 * out_id < length, hidden[c * HALF : (c + 1) * HALF], 0.0)
            total = jnp.sum(kept, axis=0, keepdims=True)
            count = jnp.full((1, CH), (length + 1) >> 1, jnp.int32).astype(jnp.float32)
            pool_f[pl.ds(clip, 1), :] = total / count

    for i in range(EARLY):
        tower_chunk(i)
    pl.semaphore_wait(barrier, len(greeted))

    def to_partner(ref, index):
        return launch(
            remote(ref.at[s], ref.at[s], pair_send.at[index], pair_recv.at[index], {"sub": other})
        )

    def from_partner(ref, index):
        here = ref.at[other]
        remote(here, here, pair_send.at[index], pair_recv.at[index], {"sub": other}).wait_recv()

    to_partner(info, 0)
    set_out(TEXT)
    to_partner(text_rows, 1)
    both_subs(text_rows.at[s], text_rows.at[2 + s], 0, up)
    for i in range(EARLY, n_chunks):
        tower_chunk(i)

    from_partner(info, 0)
    clip_text = jnp.zeros((ROWS, 1), jnp.int32)
    for h in (0, 1):
        fills = info[h, pl.ds(0, 1), pl.ds(0, ROWS)] == sub_id + s * ROWS
        texts = jnp.where(fills, info[h, pl.ds(1, 1), pl.ds(0, ROWS)], 0)
        clip_text += jnp.sum(texts, axis=1, keepdims=True)
    lane = lax.broadcasted_iota(jnp.int32, (ROWS, EXT), 1)
    extra = jnp.where(lane == 0, clip_text >> 8, jnp.where(lane == 1, clip_text & 255, 0))
    own_pooled = pool_f[...].astype(jnp.bfloat16)
    pooled[s] = own_pooled
    abuf[z, :, pl.ds(0, CH)] = own_pooled
    abuf[z, :, pl.ds(CH, EXT)] = extra.astype(jnp.float32).astype(jnp.bfloat16)
    to_partner(pooled, 2)
    set_out(AUDIO)

    relay(TEXT)

    loads["proj"].wait()
    from_partner(pooled, 2)
    pair_assign = [column(info[h, pl.ds(0, 1), pl.ds(0, ROWS)]) for h in (0, 1)]
    pair_pos = [column(info[h, pl.ds(1, 1), pl.ds(0, ROWS)]) for h in (0, 1)]
    clip_id = lax.broadcasted_iota(jnp.int32, (2 * ROWS, 2 * ROWS), 1)
    order = jnp.where(jnp.concatenate(pair_assign, axis=0) == clip_id, 1.0, 0.0)
    slots = dot_nn(order.astype(jnp.bfloat16), pooled[...].reshape(2 * ROWS, CH))
    slot_rows[pl.ds(0, 2)] = slots.astype(jnp.bfloat16).reshape(2, ROWS, CH)
    both_subs(slot_rows.at[s], slot_rows.at[2 + s], 1, down)

    relay(AUDIO)

    def embed(rows):
        return unit_rows(dot_nn(rows, projw_v[...])).astype(jnp.bfloat16)

    leaf(TEXT, 0)
    leaf(TEXT, 1)
    arrive(TEXT, -1, far)
    both_came(slot_rows, 1)
    audio = embed(slot_rows[...].reshape(4 * ROWS, CH))
    texts = zbuf[...].reshape(nz * ROWS, E)
    logits = scale * dot_nt(audio, texts) + bias
    pos = jnp.concatenate([*pair_pos, jnp.full((2 * ROWS, 1), -1, jnp.int32)], axis=0)
    text_at = lax.broadcasted_iota(jnp.int32, logits.shape, 1)
    hit = 2 * text_at - (text_at & (ROWS - 1)) + ROWS * s == pos
    grad_a = scale * dot_nn(weights_of(logits, hit), texts)
    part_a[...] = grad_a.reshape(4, ROWS, E)
    back_a[...] = grad_a.astype(jnp.bfloat16).reshape(4, ROWS, E)
    hand_back(back_a, got_a, 0, up)
    own_a[...] = part_a[s]

    from_partner(text_rows, 1)
    both_came(text_rows, 0)
    row = lax.broadcasted_iota(jnp.int32, (4 * ROWS, 1), 0)
    own_texts = text_rows[...].reshape(4 * ROWS, E)
    text_id = jnp.where(row < 2 * ROWS, 2 * ROWS * z + row, -1).astype(jnp.float32)
    ext_lane = lax.broadcasted_iota(jnp.int32, (4 * ROWS, EXT), 1)
    pos_pick = jnp.where(ext_lane == 0, 256.0, jnp.where(ext_lane == 1, 1.0, 0.0))
    pos_pick = pos_pick.astype(jnp.bfloat16)

    def text_side(offsets):
        rows = jnp.concatenate([abuf[at_z(o)] for o in offsets], axis=0)
        audio = embed(rows[:, :CH])
        logits = scale * dot_nt(own_texts, audio) + bias
        hit = dot_nt(pos_pick, rows[:, CH:]) == text_id
        return dot_nn(weights_of(logits, hit), audio)

    leaf(AUDIO, 0)
    part_t[...] = text_side([-sign1 * d for d in range(far)]).reshape(4, ROWS, E)
    leaf(AUDIO, 1)
    arrive(AUDIO, -1, far)
    rest = text_side([sign1 * d for d in range(1, far + 1)]).reshape(4, ROWS, E)
    total = scale * (part_t[...] + rest)
    part_t[...] = total
    back_t[...] = total.astype(jnp.bfloat16)
    hand_back(back_t, got_t, 1, down)
    own_t[...] = part_t[s]

    handed_back(got_a, 0)
    handed_back(got_t, 1)
    for copy in sent:
        copy.wait_send()


def add_up(own_a, own_t, got_a, got_t, ag_ref, tg_ref):
    ag_ref[...] = own_a[...] + jnp.sum(got_a[...].astype(jnp.float32), axis=0)
    tg_ref[...] = own_t[...] + jnp.sum(got_t[...].astype(jnp.float32), axis=0)


def on_device(nz, ng, clips, lengths, assign, text, positives, conv_w, proj_w, logit_scale, logit_bias):
    far = nz // 2
    smem = pl.BlockSpec(memory_space=pltpu.SMEM)
    vmem = pl.BlockSpec(memory_space=pltpu.VMEM)
    hbm = pl.BlockSpec(memory_space=pl.ANY)
    bf16, f32, dma = jnp.bfloat16, jnp.float32, pltpu.SemaphoreType.DMA
    wide = jax.ShapeDtypeStruct((ROWS, E), f32)
    short = jax.ShapeDtypeStruct((3, ROWS, E), bf16)
    parts = pl.pallas_call(
        functools.partial(kernel, nz, ng),
        out_shape=(wide, wide, short, short),
        in_specs=[smem, smem, smem, vmem, vmem, hbm, hbm, hbm, hbm],
        out_specs=(vmem, vmem, vmem, vmem),
        scratch_shapes=[
            pltpu.VMEM((ROWS, E), bf16),
            pltpu.VMEM((ROWS, FRAMES, CH), bf16),
            pltpu.VMEM((3 * CH, CH), bf16),
            pltpu.VMEM((CH, E), bf16),
            pltpu.VMEM((CHUNK * HALF, 3 * CH), bf16),
            pltpu.VMEM((ROWS, CH), f32),
            pltpu.VMEM((nz, ROWS, E), bf16),
            pltpu.VMEM((nz, ROWS, CH + EXT), bf16),
            pltpu.VMEM((4, ROWS, E), bf16),
            pltpu.VMEM((2, ROWS, CH), bf16),
            pltpu.VMEM((4, ROWS, CH), bf16),
            pltpu.VMEM((2, 8, 128), jnp.int32),
            pltpu.VMEM((4, ROWS, E), f32),
            pltpu.VMEM((4, ROWS, E), f32),
            pltpu.VMEM((4, ROWS, E), bf16),
            pltpu.VMEM((4, ROWS, E), bf16),
            dma((3 + ROWS // CHUNK,)),
            dma((3,)),
            dma((3,)),
            dma((2, 2, far)),
            dma((2, 2, far)),
            dma((2, 2)),
            dma((2, 2)),
            dma((2, 3)),
            dma((2, 3)),
        ],
        compiler_params=pltpu.CompilerParams(
            collective_id=0, has_side_effects=True, vmem_limit_bytes=67043328
        ),
        name="contrastive_step",
    )(
        logit_scale.reshape(1), logit_bias.reshape(1), lengths, assign, positives, text, clips,
        conv_w, proj_w,
    )
    return pl.pallas_call(
        add_up,
        out_shape=(wide, wide),
        in_specs=[vmem] * 4,
        out_specs=(vmem, vmem),
        name="add_up",
    )(*parts)


def solution(mesh):
    in_specs = (
        P(("grp", "blk", "sub"), None, None),
        P(("grp", "blk", "sub")),
        P(("grp", "blk"), "sub"),
        P(("grp", "blk", "sub"), None),
        P("grp", ("blk", "sub")),
        P(),
        P(),
        P(),
        P(),
    )
    out_specs = (P(("grp", "blk", "sub"), None), P(("grp", "blk", "sub"), None))
    body = functools.partial(on_device, mesh.shape["blk"], mesh.shape["grp"])
    return jax.shard_map(body, mesh=mesh, in_specs=in_specs, out_specs=out_specs, check_vma=False)
```

```python
import functools
import math

import jax
import jax.numpy as jnp
from jax import lax
from jax.experimental import pallas as pl
from jax.experimental.pallas import tpu as pltpu
from jax.sharding import PartitionSpec as P

MESH = pl.DeviceIdType.MESH
ROWS = 16
FRAMES = 128
HALF = 64
CH = 512
E = 1024
EXT = 128
TEXT, AUDIO = 0, 1
TEXT_PARENT = {1: 0, 2: 1, 3: 0, 4: 3, 5: 4, 6: 3, 7: 6, 8: 6}
AUDIO_PARENT = {1: 0, 2: 0, 3: 2, 4: 2, 5: 0, 6: 5, 7: 5, 8: 5}
CHUNK = 4


def dot_nn(a, b):
    return jnp.dot(a, b, preferred_element_type=jnp.float32)


def dot_nt(a, b):
    return lax.dot_general(a, b, (((1,), (1,)), ((), ())), preferred_element_type=jnp.float32)


def gelu(x):
    inner = math.sqrt(2.0 / math.pi) * (x + 0.044715 * (x * x * x))
    return 0.5 * x * (1.0 + jnp.tanh(inner))


def unit_rows(wide):
    return wide * lax.rsqrt(jnp.sum(wide * wide, axis=1, keepdims=True) + 1e-06)


def weights_of(logits, hit):
    signed = jnp.where(hit, -logits, logits)
    s = jax.nn.sigmoid(signed)
    return jnp.where(hit, -s, s).astype(jnp.bfloat16)


def kernel(
    nz, ng,
    scale_ref, bias_ref, len_ref, assign_ref, pos_ref, text_hbm, clips_hbm, convw_hbm, projw_hbm,
    own_a, own_t, got_a, got_t,
    text_v, clips_v, convw_v, projw_v, picked, pool_f, zbuf, abuf, text_rows, pooled, slot_rows, info,
    part_a, part_t, back_a, back_t,
    load_sem, pair_send, pair_recv, ring_send, ring_recv, rows_send, rows_recv, part_send, part_recv,
):
    g, z, s = lax.axis_index("grp"), lax.axis_index("blk"), lax.axis_index("sub")
    other = 1 - s
    up, down = lax.rem(g + 1, ng), lax.rem(g + ng - 1, ng)
    far = nz // 2
    parents = {TEXT: TEXT_PARENT, AUDIO: AUDIO_PARENT}
    bufs = {TEXT: zbuf, AUDIO: abuf}
    scale, bias = scale_ref[0], bias_ref[0]
    sign1 = jnp.where(z < far, -1, 1)
    signs = (sign1, -sign1)

    def at_z(offset):
        return lax.rem(z + offset + 2 * nz, nz)

    n_chunks = ROWS // CHUNK
    loads = {"text": pltpu.make_async_copy(text_hbm, text_v, load_sem.at[0])}
    loads["conv"] = pltpu.make_async_copy(convw_hbm, convw_v, load_sem.at[1])
    loads["proj"] = pltpu.make_async_copy(projw_hbm, projw_v, load_sem.at[2])
    for i in range(n_chunks):
        part = pl.ds(i * CHUNK, CHUNK)
        loads[i] = pltpu.make_async_copy(clips_hbm.at[part], clips_v.at[part], load_sem.at[3 + i])
    for name in ("text", 0, "conv", *range(1, n_chunks), "proj"):
        loads[name].start()

    jumps = {d - p for table in parents.values() for d, p in table.items() if d <= far}
    barrier = pltpu.get_barrier_semaphore()
    greeted = [{"sub": other}]
    greeted += [{"grp": near_group, "sub": h} for near_group in (up, down) for h in (0, 1)]
    for place in sorted({j % nz for j in jumps} | {-j % nz for j in jumps}):
        greeted.append({"blk": at_z(place)})
    for device in greeted:
        pl.semaphore_signal(barrier, inc=1, device_id=device, device_id_type=MESH)

    sent = []

    def remote(src, dst, send, recv, device):
        return pltpu.make_async_remote_copy(
            src_ref=src, dst_ref=dst, send_sem=send, recv_sem=recv, device_id=device,
            device_id_type=MESH,
        )

    def launch(copy):
        copy.start()
        sent.append(copy)
        return copy

    def ring_copy(kind, sign, d, back):
        hop = d - parents[kind][d]
        here = bufs[kind].at[at_z(-sign * (d if back else d - hop))]
        way = (1 - sign) // 2
        return remote(
            here, here, ring_send.at[kind, way, d - 1], ring_recv.at[kind, way, d - 1],
            {"blk": at_z(sign * hop)},
        )

    def arrive(kind, sign, d):
        ring_copy(kind, sign, d, True).wait_recv()

    def pass_on(kind, sign, d):
        for child in range(far - 1, d, -1):
            if parents[kind][child] == d:
                launch(ring_copy(kind, sign, child, False))

    def pass_half_way(kind, d):
        if parents[kind][far] == d:
            launch(ring_copy(kind, -1, far, False))

    def set_out(kind):
        pass_half_way(kind, 0)
        for sign in signs:
            pass_on(kind, sign, 0)

    relays = {k: sorted({p for d, p in t.items() if d <= far and p > 0}) for k, t in parents.items()}
    leaves = {k: [d for d in range(1, far) if d not in relays[k]] for k in parents}

    def relay(kind):
        for d in relays[kind]:
            for sign in signs:
                arrive(kind, sign, d)
                pass_on(kind, sign, d)
            pass_half_way(kind, d)

    def leaf(kind, index):
        for d in leaves[kind]:
            arrive(kind, signs[index], d)

    def both_subs(src, dst, sems, group):
        for h in (0, 1):
            launch(
                remote(
                    src, dst, rows_send.at[sems, h], rows_recv.at[sems, s], {"grp": group, "sub": h}
                )
            )

    def both_came(dst, sems):
        for h in (0, 1):
            here = dst.at[2 + h]
            remote(
                here, here, rows_send.at[sems, h], rows_recv.at[sems, h], {"grp": up, "sub": h}
            ).wait_recv()

    def hand_back(src, dst, sems, group):
        for h in (0, 1):
            launch(
                remote(
                    src.at[2 + h], dst.at[1 + s], part_send.at[sems, 1 + h],
                    part_recv.at[sems, 1 + s], {"grp": group, "sub": h},
                )
            )
        launch(
            remote(src.at[other], dst.at[0], part_send.at[sems, 0], part_recv.at[sems, 0], {"sub": other})
        )

    def handed_back(dst, sems):
        for i in range(3):
            here = dst.at[i]
            remote(
                here, here, part_send.at[sems, i], part_recv.at[sems, i], {"sub": other}
            ).wait_recv()

    loads["text"].wait()
    zt = unit_rows(text_v[...].astype(jnp.float32)).astype(jnp.bfloat16)
    zbuf[z] = zt
    text_rows[s] = zt
    info[s, pl.ds(0, 1), pl.ds(0, ROWS)] = assign_ref[...]
    info[s, pl.ds(1, 1), pl.ds(0, ROWS)] = pos_ref[...]
    sub_id = lax.broadcasted_iota(jnp.int32, (ROWS, ROWS), 0)
    lane_id = lax.broadcasted_iota(jnp.int32, (ROWS, ROWS), 1)

    def column(row):
        return jnp.sum(jnp.where(sub_id == lane_id, row, 0), axis=1, keepdims=True)

    frame = lax.broadcasted_iota(jnp.int32, (3 * HALF, FRAMES), 1)
    place = lax.broadcasted_iota(jnp.int32, (3 * HALF, FRAMES), 0)
    tap = (place >= HALF).astype(jnp.int32) + (place >= 2 * HALF).astype(jnp.int32)
    wanted = 2 * (place - HALF * tap) + tap - 1
    out_id = lax.broadcasted_iota(jnp.int32, (HALF, CH), 0)

    def tower_chunk(i, carry):
        part = pl.ds(i * CHUNK, CHUNK)
        pltpu.make_async_copy(clips_hbm.at[part], clips_v.at[part], load_sem.at[3 + i]).wait()
        for c in range(CHUNK):
            clip = i * CHUNK + c
            length = len_ref[clip]
            choose = jnp.where((wanted == frame) & (frame < length), 1.0, 0.0).astype(jnp.bfloat16)
            rows = dot_nn(choose, clips_v[clip]).astype(jnp.bfloat16)
            for k in range(3):
                picked[pl.ds(c * HALF, HALF), pl.ds(k * CH, CH)] = rows[k * HALF : (k + 1) * HALF]
        hidden = gelu(dot_nn(picked[...], convw_v[...]))
        for c in range(CHUNK):
            clip = i * CHUNK + c
            length = len_ref[clip]
            kept = jnp.where(2 * out_id < length, hidden[c * HALF : (c + 1) * HALF], 0.0)
            total = jnp.sum(kept, axis=0, keepdims=True)
            count = jnp.full((1, CH), (length + 1) >> 1, jnp.int32).astype(jnp.float32)
            pool_f[pl.ds(clip, 1), :] = total / count
        return carry

    early = jnp.clip((nz - 1 - z) * 4 // CHUNK, 1, n_chunks)
    loads["conv"].wait()
    lax.fori_loop(0, early, tower_chunk, 0)
    pl.semaphore_wait(barrier, len(greeted))

    def to_partner(ref, index):
        return launch(
            remote(ref.at[s], ref.at[s], pair_send.at[index], pair_recv.at[index], {"sub": other})
        )

    def from_partner(ref, index):
        here = ref.at[other]
        remote(here, here, pair_send.at[index], pair_recv.at[index], {"sub": other}).wait_recv()

    to_partner(info, 0)
    set_out(TEXT)
    to_partner(text_rows, 1)
    both_subs(text_rows.at[s], text_rows.at[2 + s], 0, up)
    lax.fori_loop(early, n_chunks, tower_chunk, 0)

    from_partner(info, 0)
    clip_text = jnp.zeros((ROWS, 1), jnp.int32)
    for h in (0, 1):
        fills = info[h, pl.ds(0, 1), pl.ds(0, ROWS)] == sub_id + s * ROWS
        texts = jnp.where(fills, info[h, pl.ds(1, 1), pl.ds(0, ROWS)], 0)
        clip_text += jnp.sum(texts, axis=1, keepdims=True)
    lane = lax.broadcasted_iota(jnp.int32, (ROWS, EXT), 1)
    extra = jnp.where(lane == 0, clip_text >> 8, jnp.where(lane == 1, clip_text & 255, 0))
    own_pooled = pool_f[...].astype(jnp.bfloat16)
    pooled[s] = own_pooled
    abuf[z, :, pl.ds(0, CH)] = own_pooled
    abuf[z, :, pl.ds(CH, EXT)] = extra.astype(jnp.float32).astype(jnp.bfloat16)
    to_partner(pooled, 2)
    set_out(AUDIO)

    relay(TEXT)

    loads["proj"].wait()
    from_partner(pooled, 2)
    pair_assign = [column(info[h, pl.ds(0, 1), pl.ds(0, ROWS)]) for h in (0, 1)]
    pair_pos = [column(info[h, pl.ds(1, 1), pl.ds(0, ROWS)]) for h in (0, 1)]
    clip_id = lax.broadcasted_iota(jnp.int32, (2 * ROWS, 2 * ROWS), 1)
    order = jnp.where(jnp.concatenate(pair_assign, axis=0) == clip_id, 1.0, 0.0)
    slots = dot_nn(order.astype(jnp.bfloat16), pooled[...].reshape(2 * ROWS, CH))
    slot_rows[pl.ds(0, 2)] = slots.astype(jnp.bfloat16).reshape(2, ROWS, CH)
    both_subs(slot_rows.at[s], slot_rows.at[2 + s], 1, down)

    relay(AUDIO)

    def embed(rows):
        return unit_rows(dot_nn(rows, projw_v[...])).astype(jnp.bfloat16)

    leaf(TEXT, 0)
    leaf(TEXT, 1)
    arrive(TEXT, -1, far)
    both_came(slot_rows, 1)
    audio = embed(slot_rows[...].reshape(4 * ROWS, CH))
    texts = zbuf[...].reshape(nz * ROWS, E)
    logits = scale * dot_nt(audio, texts) + bias
    pos = jnp.concatenate([*pair_pos, jnp.full((2 * ROWS, 1), -1, jnp.int32)], axis=0)
    text_at = lax.broadcasted_iota(jnp.int32, logits.shape, 1)
    hit = 2 * text_at - (text_at & (ROWS - 1)) + ROWS * s == pos
    grad_a = scale * dot_nn(weights_of(logits, hit), texts)
    part_a[...] = grad_a.reshape(4, ROWS, E)
    back_a[...] = grad_a.astype(jnp.bfloat16).reshape(4, ROWS, E)
    hand_back(back_a, got_a, 0, up)
    own_a[...] = part_a[s]

    from_partner(text_rows, 1)
    both_came(text_rows, 0)
    row = lax.broadcasted_iota(jnp.int32, (4 * ROWS, 1), 0)
    own_texts = text_rows[...].reshape(4 * ROWS, E)
    text_id = jnp.where(row < 2 * ROWS, 2 * ROWS * z + row, -1).astype(jnp.float32)
    ext_lane = lax.broadcasted_iota(jnp.int32, (4 * ROWS, EXT), 1)
    pos_pick = jnp.where(ext_lane == 0, 256.0, jnp.where(ext_lane == 1, 1.0, 0.0))
    pos_pick = pos_pick.astype(jnp.bfloat16)

    def text_side(offsets):
        rows = jnp.concatenate([abuf[at_z(o)] for o in offsets], axis=0)
        audio = embed(rows[:, :CH])
        logits = scale * dot_nt(own_texts, audio) + bias
        hit = dot_nt(pos_pick, rows[:, CH:]) == text_id
        return dot_nn(weights_of(logits, hit), audio)

    leaf(AUDIO, 0)
    part_t[...] = text_side([-sign1 * d for d in range(far)]).reshape(4, ROWS, E)
    leaf(AUDIO, 1)
    arrive(AUDIO, -1, far)
    rest = text_side([sign1 * d for d in range(1, far + 1)]).reshape(4, ROWS, E)
    total = scale * (part_t[...] + rest)
    part_t[...] = total
    back_t[...] = total.astype(jnp.bfloat16)
    hand_back(back_t, got_t, 1, down)
    own_t[...] = part_t[s]

    handed_back(got_a, 0)
    handed_back(got_t, 1)
    for copy in sent:
        copy.wait_send()


def add_up(own_a, own_t, got_a, got_t, ag_ref, tg_ref):
    ag_ref[...] = own_a[...] + jnp.sum(got_a[...].astype(jnp.float32), axis=0)
    tg_ref[...] = own_t[...] + jnp.sum(got_t[...].astype(jnp.float32), axis=0)


def on_device(nz, ng, clips, lengths, assign, text, positives, conv_w, proj_w, logit_scale, logit_bias):
    far = nz // 2
    smem = pl.BlockSpec(memory_space=pltpu.SMEM)
    vmem = pl.BlockSpec(memory_space=pltpu.VMEM)
    hbm = pl.BlockSpec(memory_space=pl.ANY)
    bf16, f32, dma = jnp.bfloat16, jnp.float32, pltpu.SemaphoreType.DMA
    wide = jax.ShapeDtypeStruct((ROWS, E), f32)
    short = jax.ShapeDtypeStruct((3, ROWS, E), bf16)
    parts = pl.pallas_call(
        functools.partial(kernel, nz, ng),
        out_shape=(wide, wide, short, short),
        in_specs=[smem, smem, smem, vmem, vmem, hbm, hbm, hbm, hbm],
        out_specs=(vmem, vmem, vmem, vmem),
        scratch_shapes=[
            pltpu.VMEM((ROWS, E), bf16),
            pltpu.VMEM((ROWS, FRAMES, CH), bf16),
            pltpu.VMEM((3 * CH, CH), bf16),
            pltpu.VMEM((CH, E), bf16),
            pltpu.VMEM((CHUNK * HALF, 3 * CH), bf16),
            pltpu.VMEM((ROWS, CH), f32),
            pltpu.VMEM((nz, ROWS, E), bf16),
            pltpu.VMEM((nz, ROWS, CH + EXT), bf16),
            pltpu.VMEM((4, ROWS, E), bf16),
            pltpu.VMEM((2, ROWS, CH), bf16),
            pltpu.VMEM((4, ROWS, CH), bf16),
            pltpu.VMEM((2, 8, 128), jnp.int32),
            pltpu.VMEM((4, ROWS, E), f32),
            pltpu.VMEM((4, ROWS, E), f32),
            pltpu.VMEM((4, ROWS, E), bf16),
            pltpu.VMEM((4, ROWS, E), bf16),
            dma((3 + ROWS // CHUNK,)),
            dma((3,)),
            dma((3,)),
            dma((2, 2, far)),
            dma((2, 2, far)),
            dma((2, 2)),
            dma((2, 2)),
            dma((2, 3)),
            dma((2, 3)),
        ],
        compiler_params=pltpu.CompilerParams(
            collective_id=0, has_side_effects=True, vmem_limit_bytes=67043328
        ),
        name="contrastive_step",
    )(
        logit_scale.reshape(1), logit_bias.reshape(1), lengths, assign, positives, text, clips,
        conv_w, proj_w,
    )
    return pl.pallas_call(
        add_up,
        out_shape=(wide, wide),
        in_specs=[vmem] * 4,
        out_specs=(vmem, vmem),
        name="add_up",
    )(*parts)


def solution(mesh):
    in_specs = (
        P(("grp", "blk", "sub"), None, None),
        P(("grp", "blk", "sub")),
        P(("grp", "blk"), "sub"),
        P(("grp", "blk", "sub"), None),
        P("grp", ("blk", "sub")),
        P(),
        P(),
        P(),
        P(),
    )
    out_specs = (P(("grp", "blk", "sub"), None), P(("grp", "blk", "sub"), None))
    body = functools.partial(on_device, mesh.shape["blk"], mesh.shape["grp"])
    return jax.shard_map(body, mesh=mesh, in_specs=in_specs, out_specs=out_specs, check_vma=False)
```

```python
import functools
import math

import jax
import jax.numpy as jnp
from jax import lax
from jax.experimental import pallas as pl
from jax.experimental.pallas import tpu as pltpu
from jax.sharding import PartitionSpec as P

MESH = pl.DeviceIdType.MESH
ROWS = 16
FRAMES = 128
HALF = 64
CH = 512
E = 1024
EXT = 128
TEXT, AUDIO = 0, 1
TEXT_PARENT = {1: 0, 2: 1, 3: 0, 4: 3, 5: 4, 6: 3, 7: 6, 8: 6}
AUDIO_PARENT = {1: 0, 2: 0, 3: 2, 4: 2, 5: 0, 6: 5, 7: 5, 8: 5}
HALF_WAY = {TEXT: 1, AUDIO: -1}
CHUNK = 4


def dot_nn(a, b):
    return jnp.dot(a, b, preferred_element_type=jnp.float32)


def dot_nt(a, b):
    return lax.dot_general(a, b, (((1,), (1,)), ((), ())), preferred_element_type=jnp.float32)


def gelu(x):
    inner = math.sqrt(2.0 / math.pi) * (x + 0.044715 * (x * x * x))
    return 0.5 * x * (1.0 + jnp.tanh(inner))


def unit_rows(wide):
    return wide * lax.rsqrt(jnp.sum(wide * wide, axis=1, keepdims=True) + 1e-06)


def weights_of(logits, hit):
    signed = jnp.where(hit, -logits, logits)
    s = jax.nn.sigmoid(signed)
    return jnp.where(hit, -s, s).astype(jnp.bfloat16)


def kernel(
    nz, ng,
    scale_ref, bias_ref, len_ref, assign_ref, pos_ref, text_hbm, clips_hbm, convw_hbm, projw_hbm,
    own_a, own_t, got_a, got_t,
    text_v, clips_v, convw_v, projw_v, picked, pool_f, zbuf, abuf, text_rows, pooled, slot_rows, info,
    part_a, part_t, back_a, back_t,
    load_sem, pair_send, pair_recv, ring_send, ring_recv, rows_send, rows_recv, part_send, part_recv,
):
    g, z, s = lax.axis_index("grp"), lax.axis_index("blk"), lax.axis_index("sub")
    other = 1 - s
    up, down = lax.rem(g + 1, ng), lax.rem(g + ng - 1, ng)
    far = nz // 2
    parents = {TEXT: TEXT_PARENT, AUDIO: AUDIO_PARENT}
    bufs = {TEXT: zbuf, AUDIO: abuf}
    scale, bias = scale_ref[0], bias_ref[0]
    sign1 = jnp.where(z < far, -1, 1)
    signs = (sign1, -sign1)

    def at_z(offset):
        return lax.rem(z + offset + 2 * nz, nz)

    n_chunks = ROWS // CHUNK
    loads = {"text": pltpu.make_async_copy(text_hbm, text_v, load_sem.at[0])}
    loads["conv"] = pltpu.make_async_copy(convw_hbm, convw_v, load_sem.at[1])
    loads["proj"] = pltpu.make_async_copy(projw_hbm, projw_v, load_sem.at[2])
    for i in range(n_chunks):
        part = pl.ds(i * CHUNK, CHUNK)
        loads[i] = pltpu.make_async_copy(clips_hbm.at[part], clips_v.at[part], load_sem.at[3 + i])
    for name in ("text", 0, "conv", *range(1, n_chunks), "proj"):
        loads[name].start()

    jumps = {d - p for table in parents.values() for d, p in table.items() if d <= far}
    barrier = pltpu.get_barrier_semaphore()
    greeted = [{"sub": other}]
    greeted += [{"grp": near_group, "sub": h} for near_group in (up, down) for h in (0, 1)]
    for place in sorted({j % nz for j in jumps} | {-j % nz for j in jumps}):
        greeted.append({"blk": at_z(place)})
    for device in greeted:
        pl.semaphore_signal(barrier, inc=1, device_id=device, device_id_type=MESH)

    sent = []

    def remote(src, dst, send, recv, device):
        return pltpu.make_async_remote_copy(
            src_ref=src, dst_ref=dst, send_sem=send, recv_sem=recv, device_id=device,
            device_id_type=MESH,
        )

    def launch(copy):
        copy.start()
        sent.append(copy)
        return copy

    def ring_copy(kind, sign, d, back):
        hop = d - parents[kind][d]
        here = bufs[kind].at[at_z(-sign * (d if back else d - hop))]
        way = (1 - sign) // 2
        return remote(
            here, here, ring_send.at[kind, way, d - 1], ring_recv.at[kind, way, d - 1],
            {"blk": at_z(sign * hop)},
        )

    def arrive(kind, sign, d):
        ring_copy(kind, sign, d, True).wait_recv()

    def pass_on(kind, sign, d):
        for child in range(far - 1, d, -1):
            if parents[kind][child] == d:
                launch(ring_copy(kind, sign, child, False))

    def pass_half_way(kind, d):
        if parents[kind][far] == d:
            launch(ring_copy(kind, HALF_WAY[kind], far, False))

    def set_out(kind):
        pass_half_way(kind, 0)
        for sign in signs:
            pass_on(kind, sign, 0)

    relays = {k: sorted({p for d, p in t.items() if d <= far and p > 0}) for k, t in parents.items()}
    leaves = {k: [d for d in range(1, far) if d not in relays[k]] for k in parents}

    def relay(kind):
        for d in relays[kind]:
            for sign in signs:
                arrive(kind, sign, d)
                pass_on(kind, sign, d)
            pass_half_way(kind, d)

    def leaf(kind, index):
        for d in leaves[kind]:
            arrive(kind, signs[index], d)

    def both_subs(src, dst, sems, group):
        for h in (0, 1):
            launch(
                remote(
                    src, dst, rows_send.at[sems, h], rows_recv.at[sems, s], {"grp": group, "sub": h}
                )
            )

    def both_came(dst, sems):
        for h in (0, 1):
            here = dst.at[2 + h]
            remote(
                here, here, rows_send.at[sems, h], rows_recv.at[sems, h], {"grp": up, "sub": h}
            ).wait_recv()

    def hand_back(src, dst, sems, group):
        for h in (0, 1):
            launch(
                remote(
                    src.at[2 + h], dst.at[1 + s], part_send.at[sems, 1 + h],
                    part_recv.at[sems, 1 + s], {"grp": group, "sub": h},
                )
            )
        launch(
            remote(src.at[other], dst.at[0], part_send.at[sems, 0], part_recv.at[sems, 0], {"sub": other})
        )

    def handed_back(dst, sems):
        for i in range(3):
            here = dst.at[i]
            remote(
                here, here, part_send.at[sems, i], part_recv.at[sems, i], {"sub": other}
            ).wait_recv()

    loads["text"].wait()
    zt = unit_rows(text_v[...].astype(jnp.float32)).astype(jnp.bfloat16)
    zbuf[z] = zt
    text_rows[s] = zt
    info[s, pl.ds(0, 1), pl.ds(0, ROWS)] = assign_ref[...]
    info[s, pl.ds(1, 1), pl.ds(0, ROWS)] = pos_ref[...]
    sub_id = lax.broadcasted_iota(jnp.int32, (ROWS, ROWS), 0)
    lane_id = lax.broadcasted_iota(jnp.int32, (ROWS, ROWS), 1)

    def column(row):
        return jnp.sum(jnp.where(sub_id == lane_id, row, 0), axis=1, keepdims=True)

    frame = lax.broadcasted_iota(jnp.int32, (3 * HALF, FRAMES), 1)
    place = lax.broadcasted_iota(jnp.int32, (3 * HALF, FRAMES), 0)
    tap = (place >= HALF).astype(jnp.int32) + (place >= 2 * HALF).astype(jnp.int32)
    wanted = 2 * (place - HALF * tap) + tap - 1
    out_id = lax.broadcasted_iota(jnp.int32, (HALF, CH), 0)

    def tower_chunk(i, carry):
        part = pl.ds(i * CHUNK, CHUNK)
        pltpu.make_async_copy(clips_hbm.at[part], clips_v.at[part], load_sem.at[3 + i]).wait()
        for c in range(CHUNK):
            clip = i * CHUNK + c
            length = len_ref[clip]
            choose = jnp.where((wanted == frame) & (frame < length), 1.0, 0.0).astype(jnp.bfloat16)
            rows = dot_nn(choose, clips_v[clip]).astype(jnp.bfloat16)
            for k in range(3):
                picked[pl.ds(c * HALF, HALF), pl.ds(k * CH, CH)] = rows[k * HALF : (k + 1) * HALF]
        hidden = gelu(dot_nn(picked[...], convw_v[...]))
        for c in range(CHUNK):
            clip = i * CHUNK + c
            length = len_ref[clip]
            kept = jnp.where(2 * out_id < length, hidden[c * HALF : (c + 1) * HALF], 0.0)
            total = jnp.sum(kept, axis=0, keepdims=True)
            count = jnp.full((1, CH), (length + 1) >> 1, jnp.int32).astype(jnp.float32)
            pool_f[pl.ds(clip, 1), :] = total / count
        return carry

    early = jnp.clip((nz - 1 - z) * 4 // CHUNK, 1, n_chunks)
    loads["conv"].wait()
    lax.fori_loop(0, early, tower_chunk, 0)
    pl.semaphore_wait(barrier, len(greeted))

    def to_partner(ref, index):
        return launch(
            remote(ref.at[s], ref.at[s], pair_send.at[index], pair_recv.at[index], {"sub": other})
        )

    def from_partner(ref, index):
        here = ref.at[other]
        remote(here, here, pair_send.at[index], pair_recv.at[index], {"sub": other}).wait_recv()

    to_partner(info, 0)
    set_out(TEXT)
    to_partner(text_rows, 1)
    both_subs(text_rows.at[s], text_rows.at[2 + s], 0, up)
    lax.fori_loop(early, n_chunks, tower_chunk, 0)

    from_partner(info, 0)
    clip_text = jnp.zeros((ROWS, 1), jnp.int32)
    for h in (0, 1):
        fills = info[h, pl.ds(0, 1), pl.ds(0, ROWS)] == sub_id + s * ROWS
        texts = jnp.where(fills, info[h, pl.ds(1, 1), pl.ds(0, ROWS)], 0)
        clip_text += jnp.sum(texts, axis=1, keepdims=True)
    lane = lax.broadcasted_iota(jnp.int32, (ROWS, EXT), 1)
    extra = jnp.where(lane == 0, clip_text >> 8, jnp.where(lane == 1, clip_text & 255, 0))
    own_pooled = pool_f[...].astype(jnp.bfloat16)
    pooled[s] = own_pooled
    abuf[z, :, pl.ds(0, CH)] = own_pooled
    abuf[z, :, pl.ds(CH, EXT)] = extra.astype(jnp.float32).astype(jnp.bfloat16)
    to_partner(pooled, 2)
    set_out(AUDIO)

    relay(TEXT)

    loads["proj"].wait()
    from_partner(pooled, 2)
    pair_assign = [column(info[h, pl.ds(0, 1), pl.ds(0, ROWS)]) for h in (0, 1)]
    pair_pos = [column(info[h, pl.ds(1, 1), pl.ds(0, ROWS)]) for h in (0, 1)]
    clip_id = lax.broadcasted_iota(jnp.int32, (2 * ROWS, 2 * ROWS), 1)
    order = jnp.where(jnp.concatenate(pair_assign, axis=0) == clip_id, 1.0, 0.0)
    slots = dot_nn(order.astype(jnp.bfloat16), pooled[...].reshape(2 * ROWS, CH))
    slot_rows[pl.ds(0, 2)] = slots.astype(jnp.bfloat16).reshape(2, ROWS, CH)
    both_subs(slot_rows.at[s], slot_rows.at[2 + s], 1, down)

    relay(AUDIO)

    def embed(rows):
        return unit_rows(dot_nn(rows, projw_v[...])).astype(jnp.bfloat16)

    leaf(TEXT, 0)
    leaf(TEXT, 1)
    arrive(TEXT, HALF_WAY[TEXT], far)
    both_came(slot_rows, 1)
    audio = embed(slot_rows[...].reshape(4 * ROWS, CH))
    texts = zbuf[...].reshape(nz * ROWS, E)
    logits = scale * dot_nt(audio, texts) + bias
    pos = jnp.concatenate([*pair_pos, jnp.full((2 * ROWS, 1), -1, jnp.int32)], axis=0)
    text_at = lax.broadcasted_iota(jnp.int32, logits.shape, 1)
    hit = 2 * text_at - (text_at & (ROWS - 1)) + ROWS * s == pos
    grad_a = scale * dot_nn(weights_of(logits, hit), texts)
    part_a[...] = grad_a.reshape(4, ROWS, E)
    back_a[...] = grad_a.astype(jnp.bfloat16).reshape(4, ROWS, E)
    hand_back(back_a, got_a, 0, up)
    own_a[...] = part_a[s]

    from_partner(text_rows, 1)
    both_came(text_rows, 0)
    row = lax.broadcasted_iota(jnp.int32, (4 * ROWS, 1), 0)
    own_texts = text_rows[...].reshape(4 * ROWS, E)
    text_id = jnp.where(row < 2 * ROWS, 2 * ROWS * z + row, -1).astype(jnp.float32)
    ext_lane = lax.broadcasted_iota(jnp.int32, (4 * ROWS, EXT), 1)
    pos_pick = jnp.where(ext_lane == 0, 256.0, jnp.where(ext_lane == 1, 1.0, 0.0))
    pos_pick = pos_pick.astype(jnp.bfloat16)

    def text_side(offsets):
        rows = jnp.concatenate([abuf[at_z(o)] for o in offsets], axis=0)
        audio = embed(rows[:, :CH])
        logits = scale * dot_nt(own_texts, audio) + bias
        hit = dot_nt(pos_pick, rows[:, CH:]) == text_id
        return dot_nn(weights_of(logits, hit), audio)

    leaf(AUDIO, 0)
    part_t[...] = text_side([-sign1 * d for d in range(far)]).reshape(4, ROWS, E)
    leaf(AUDIO, 1)
    arrive(AUDIO, HALF_WAY[AUDIO], far)
    rest = text_side([sign1 * d for d in range(1, far + 1)]).reshape(4, ROWS, E)
    total = scale * (part_t[...] + rest)
    part_t[...] = total
    back_t[...] = total.astype(jnp.bfloat16)
    hand_back(back_t, got_t, 1, down)
    own_t[...] = part_t[s]

    handed_back(got_a, 0)
    handed_back(got_t, 1)
    for copy in sent:
        copy.wait_send()


def add_up(own_a, own_t, got_a, got_t, ag_ref, tg_ref):
    ag_ref[...] = own_a[...] + jnp.sum(got_a[...].astype(jnp.float32), axis=0)
    tg_ref[...] = own_t[...] + jnp.sum(got_t[...].astype(jnp.float32), axis=0)


def on_device(nz, ng, clips, lengths, assign, text, positives, conv_w, proj_w, logit_scale, logit_bias):
    far = nz // 2
    smem = pl.BlockSpec(memory_space=pltpu.SMEM)
    vmem = pl.BlockSpec(memory_space=pltpu.VMEM)
    hbm = pl.BlockSpec(memory_space=pl.ANY)
    bf16, f32, dma = jnp.bfloat16, jnp.float32, pltpu.SemaphoreType.DMA
    wide = jax.ShapeDtypeStruct((ROWS, E), f32)
    short = jax.ShapeDtypeStruct((3, ROWS, E), bf16)
    parts = pl.pallas_call(
        functools.partial(kernel, nz, ng),
        out_shape=(wide, wide, short, short),
        in_specs=[smem, smem, smem, vmem, vmem, hbm, hbm, hbm, hbm],
        out_specs=(vmem, vmem, vmem, vmem),
        scratch_shapes=[
            pltpu.VMEM((ROWS, E), bf16),
            pltpu.VMEM((ROWS, FRAMES, CH), bf16),
            pltpu.VMEM((3 * CH, CH), bf16),
            pltpu.VMEM((CH, E), bf16),
            pltpu.VMEM((CHUNK * HALF, 3 * CH), bf16),
            pltpu.VMEM((ROWS, CH), f32),
            pltpu.VMEM((nz, ROWS, E), bf16),
            pltpu.VMEM((nz, ROWS, CH + EXT), bf16),
            pltpu.VMEM((4, ROWS, E), bf16),
            pltpu.VMEM((2, ROWS, CH), bf16),
            pltpu.VMEM((4, ROWS, CH), bf16),
            pltpu.VMEM((2, 8, 128), jnp.int32),
            pltpu.VMEM((4, ROWS, E), f32),
            pltpu.VMEM((4, ROWS, E), f32),
            pltpu.VMEM((4, ROWS, E), bf16),
            pltpu.VMEM((4, ROWS, E), bf16),
            dma((3 + ROWS // CHUNK,)),
            dma((3,)),
            dma((3,)),
            dma((2, 2, far)),
            dma((2, 2, far)),
            dma((2, 2)),
            dma((2, 2)),
            dma((2, 3)),
            dma((2, 3)),
        ],
        compiler_params=pltpu.CompilerParams(
            collective_id=0, has_side_effects=True, vmem_limit_bytes=67043328
        ),
        name="contrastive_step",
    )(
        logit_scale.reshape(1), logit_bias.reshape(1), lengths, assign, positives, text, clips,
        conv_w, proj_w,
    )
    return pl.pallas_call(
        add_up,
        out_shape=(wide, wide),
        in_specs=[vmem] * 4,
        out_specs=(vmem, vmem),
        name="add_up",
    )(*parts)


def solution(mesh):
    in_specs = (
        P(("grp", "blk", "sub"), None, None),
        P(("grp", "blk", "sub")),
        P(("grp", "blk"), "sub"),
        P(("grp", "blk", "sub"), None),
        P("grp", ("blk", "sub")),
        P(),
        P(),
        P(),
        P(),
    )
    out_specs = (P(("grp", "blk", "sub"), None), P(("grp", "blk", "sub"), None))
    body = functools.partial(on_device, mesh.shape["blk"], mesh.shape["grp"])
    return jax.shard_map(body, mesh=mesh, in_specs=in_specs, out_specs=out_specs, check_vma=False)
```
